32 devices in a mesh: section: 4 (over y, x), vocab: 8 (over z, core).
Axes of the slice: x: 2, y: 2, z: 4, core: 2. Of those that a mesh axis runs over, the one named last changes fastest.
Arguments:
- exit_hidden: bfloat16 [3, 256, 8192], P(None, 'vocab', 'section')
- norm_gain: float32 [3, 8192], P(None, 'section'), may hold values from 0.5 to 1.5
- head_weight: bfloat16 [8192, 65536], P(None, ('section', 'vocab'))
- teacher: float32 [256, 65536], P('vocab', 'section'), as said below
Outputs:
- divergence: float32 [3], replicated
- grad_hidden: bfloat16 [3, 256, 8192], P(None, 'vocab', 'section')
- grad_head: bfloat16 [8192, 65536], P(None, ('section', 'vocab'))
The draws below stay inside these ranges and needn't reach their ends.
Inputs may be any that keep to these rules, and one draw needn't show every extreme that they name: Each row of teacher holds log-probabilities: their exponentials sum to one.
All inputs are finite; a program needn't handle non-finite values.
Results may differ from the reference program's by a relative error of at most 0.0086.
Values may be sent and summed in bfloat16 or wider, within the bound.
No kernel may reach another device: no remote copies, remote signals or barrier semaphores. Data moves between devices by JAX's collectives and lax.ppermute only.
A program may use at most 192 MiB of HBM per device.

```python
import math
import jax
import jax.numpy as jnp
from jax import lax

D = 8192
VOCAB = 65536
EXITS = 3
TOK = 256


def draw_exit_hidden(key, part):
    shape = (EXITS, TOK, D)
    ramp = 3.0 ** (jnp.arange(D, dtype=jnp.float32) / D)
    col_scale = jnp.exp(jax.random.uniform(jax.random.fold_in(key, 2), (1, 1, D), minval=0.0, maxval=math.log(2.0))) * ramp
    row_scale = jnp.exp(jax.random.uniform(jax.random.fold_in(key, 1), (EXITS, TOK, 1), minval=0.0, maxval=math.log(10.0)))
    values = jax.random.normal(jax.random.fold_in(key, 3), shape) * row_scale * col_scale
    return values.astype(jnp.bfloat16)


def draw_head_weight(key, part):
    scale = 3.0 / math.sqrt(D)
    values = jax.random.normal(jax.random.fold_in(key, 1), (D, VOCAB)) * scale
    return values.astype(jnp.bfloat16)


def draw_teacher(key, part):
    raw = jax.random.normal(jax.random.fold_in(key, 5), (TOK, VOCAB)) * 3.0
    return jax.nn.log_softmax(raw, axis=-1).astype(jnp.float32)


def setup_inputs(seed: int = 0) -> dict:
    splits = jax.random.split(jax.random.key(seed), 5)
    return {
        "exit_hidden": draw_exit_hidden(jax.random.fold_in(splits[4], 71), 0),
        "norm_gain": jnp.clip(1.0 + 0.1 * jax.random.normal(splits[1], (EXITS, D), jnp.float32), 0.5, 1.5),
        "head_weight": draw_head_weight(jax.random.fold_in(splits[4], 71), 0),
        "teacher": draw_teacher(jax.random.fold_in(splits[4], 71), 0),
    }


epsilon = 1e-05
loss_scale = 1024.0

def reference(exit_hidden, norm_gain, head_weight, teacher):
    hidden = exit_hidden.astype(jnp.float32)
    gains = norm_gain.astype(jnp.float32)[:, None, :]
    squares = lax.optimization_barrier(jnp.sum(hidden * hidden, axis=-1, keepdims=True))
    inverse = lax.rsqrt(squares / D + epsilon)
    normed = (hidden * inverse * gains).astype(jnp.bfloat16)
    flat_rows = normed.reshape(EXITS * TOK, D)
    logits = jnp.dot(flat_rows, head_weight, preferred_element_type=jnp.float32).reshape(EXITS, TOK, VOCAB)
    row_max = lax.optimization_barrier(jnp.max(logits, axis=-1))
    log_total = row_max + jnp.log(lax.optimization_barrier(jnp.sum(jnp.exp(logits - row_max[..., None]), axis=-1)))
    target = jnp.exp(teacher)[None]
    cross = lax.optimization_barrier(jnp.sum(target * (teacher[None] - logits), axis=-1))
    weight_sum = lax.optimization_barrier(jnp.sum(target, axis=-1))
    divergence = lax.optimization_barrier(jnp.mean(cross + log_total * weight_sum, axis=-1))
    dlogit = ((jnp.exp(logits - log_total[..., None]) - target) * (loss_scale / TOK)).astype(jnp.bfloat16)
    flat_dlogit = dlogit.reshape(EXITS * TOK, VOCAB)
    grad_head = jnp.dot(flat_rows.T, flat_dlogit, preferred_element_type=jnp.float32).astype(jnp.bfloat16)
    grad_normed = jnp.dot(flat_dlogit, head_weight.T, preferred_element_type=jnp.float32).reshape(EXITS, TOK, D)
    weighted = gains * grad_normed
    inner = lax.optimization_barrier(jnp.sum(weighted * hidden, axis=-1, keepdims=True))
    grad_hidden = (inverse * weighted - hidden * inverse ** 3 * inner / D).astype(jnp.bfloat16)
    return (divergence, grad_hidden, grad_head)
```

```python
import functools
import jax
import jax.numpy as jnp
from jax import lax
from jax.experimental import pallas as pl
from jax.experimental.pallas import tpu as pltpu
from jax.sharding import PartitionSpec as P

epsilon = 1e-05
loss_scale = 1024.0
F32 = jnp.float32
BF16 = jnp.bfloat16
LANES = 128


def swap(x, axis, mask, size):
    return lax.ppermute(x, axis, [(i, i ^ mask) for i in range(size)])


def low(o):
    return o & -o


def high(o):
    return 1 << (o.bit_length() - 1)


def route(o, k):
    return low(o) if k & 1 else high(o)


def gather_order(sections, chips):
    single = [o for o in range(1, sections) if o.bit_count() == 1]
    several = sorted(
        (o for o in range(1, sections) if o.bit_count() > 1), key=lambda o: (o.bit_count(), o)
    )
    seq = []
    for k in range(chips + 1):
        if k < chips:
            seq += [("z", 0, c) for c in range(1, chips) if c ^ low(c) == k]
            seq += [("s", o, k) for o in single]
        if k:
            seq += [("s", o, k - 1) for o in several]
    return seq


def reduce_order(sections, chips):
    return [
        (o, k)
        for count in range(sections.bit_length() - 1, 0, -1)
        for k in reversed(range(chips))
        for o in range(1, sections)
        if o.bit_count() == count
    ]


def merge_kernel(masks, log, *refs):
    own, others, out = refs[0], refs[1:-1], refs[-1]
    n = own.shape[1]
    for b in range(n):
        row = pl.ds(b, 1)
        sources = [(own, row)] + [(r, pl.ds(b ^ m, 1)) for r, m in zip(others, masks)]
        tops = [r[0, at, :] for r, at in sources]
        top = functools.reduce(jnp.maximum, tops)
        total = functools.reduce(
            jnp.add, [r[1, at, :] * jnp.exp(t - top) for (r, at), t in zip(sources, tops)]
        )
        if log:
            out[row, :] = top + jnp.log(total)
        else:
            out[0, row, :] = top
            out[1, row, :] = total


def merge(own, others, masks, log=False):
    return pl.pallas_call(
        functools.partial(merge_kernel, masks, log),
        out_shape=jax.ShapeDtypeStruct(own.shape[1:] if log else own.shape, F32),
        compiler_params=pltpu.CompilerParams(vmem_limit_bytes=4 << 20),
        name="merge",
    )(own, *others)


def logits_kernel(offsets, n_blocks, has_acc, last, *refs):
    n = len(offsets)
    refs = refs[1:]
    pieces, refs = refs[: n * n_blocks], refs[n * n_blocks :]
    weights, refs = refs[:n], refs[n:]
    acc_ref = None
    if has_acc:
        acc_ref, refs = refs[0], refs[1:]
    out_ref, states_ref, stat_ref, refs = refs[0], refs[1], refs[2], refs[3:]
    lhs, in_sem, out_sem = refs[:3]
    rows = pieces[0].shape[0]
    step = pl.program_id(0)
    final = pl.num_programs(0) - 1

    def incoming(g, b):
        return pltpu.make_async_copy(
            pieces[g * n_blocks + b], lhs.at[g, pl.ds(b * rows, rows), :], in_sem.at[g, b]
        )

    def outgoing(g):
        return pltpu.make_async_copy(lhs.at[g], states_ref.at[g], out_sem.at[g])

    @pl.when(step == 0)
    def _():
        for g in range(n):
            for b in range(n_blocks):
                incoming(g, b).start()
        for g in range(n):
            for b in range(n_blocks):
                incoming(g, b).wait()
        for g in range(n):
            outgoing(g).start()

    total = acc_ref[...] if has_acc else None
    for g in range(n):
        part = jnp.dot(lhs[g], weights[g][...], preferred_element_type=F32)
        total = part if total is None else total + part
    out_ref[...] = total
    if last:
        max_ref, sum_ref = refs[3:]
        block_max = jnp.max(total, axis=1, keepdims=True)

        @pl.when(step == 0)
        def _():
            max_ref[...] = jnp.broadcast_to(block_max, max_ref.shape)
            sum_ref[...] = jnp.zeros_like(sum_ref)

        old = max_ref[:, :1]
        new = jnp.maximum(old, block_max)
        fresh = sum_ref[:, :1] * jnp.exp(old - new) + jnp.sum(
            jnp.exp(total - new), axis=1, keepdims=True
        )
        max_ref[...] = jnp.broadcast_to(new, max_ref.shape)
        sum_ref[...] = jnp.broadcast_to(fresh, sum_ref.shape)

    @pl.when(step == final)
    def _():
        for g in range(n):
            outgoing(g).wait()
        if not last:
            stat_ref[...] = jnp.zeros_like(stat_ref)
        else:
            pad = jnp.ones((LANES - rows, LANES), F32)
            for b in range(n_blocks):
                for plane, ref in enumerate((max_ref, sum_ref)):
                    tile = jnp.concatenate([ref[pl.ds(b * rows, rows), :], pad], axis=0)
                    stat_ref[plane, pl.ds(b, 1), :] = tile.T[:1, :]


def logits_part(offsets, position, pieces, weight, acc, last):
    n, n_blocks = len(offsets), len(pieces[0])
    rows, depth = pieces[0][0].shape
    total_rows = n_blocks * rows
    local = weight.shape[1]
    tile = min(512, local)
    any_spec = pl.BlockSpec(memory_space=pl.ANY)
    block = pl.BlockSpec((total_rows, tile), lambda i, pos: (0, i))

    def weight_spec(offset):
        return pl.BlockSpec((depth, tile), lambda i, pos: (pos[offset], i))

    operands = [p for group in pieces for p in group] + [weight] * n
    in_specs = [any_spec] * (n * n_blocks) + [weight_spec(o) for o in offsets]
    if acc is not None:
        operands.append(acc)
        in_specs.append(block)
    out_shape = [
        jax.ShapeDtypeStruct((total_rows, local), F32),
        jax.ShapeDtypeStruct((n, total_rows, depth), BF16),
        jax.ShapeDtypeStruct((2, n_blocks, LANES), F32),
    ]
    out_specs = [block, any_spec, pl.BlockSpec((2, n_blocks, LANES), lambda i, pos: (0, 0, 0))]
    scratch = [
        pltpu.VMEM((n, total_rows, depth), BF16),
        pltpu.SemaphoreType.DMA((n, n_blocks)),
        pltpu.SemaphoreType.DMA((n,)),
    ]
    if last:
        scratch += [pltpu.VMEM((total_rows, LANES), F32)] * 2
    return pl.pallas_call(
        functools.partial(logits_kernel, offsets, n_blocks, acc is not None, last),
        grid_spec=pltpu.PrefetchScalarGridSpec(
            num_scalar_prefetch=1,
            grid=(local // tile,),
            in_specs=in_specs,
            out_specs=out_specs,
            scratch_shapes=scratch,
        ),
        out_shape=out_shape,
        compiler_params=pltpu.CompilerParams(vmem_limit_bytes=32 << 20),
        cost_estimate=pl.CostEstimate(
            flops=2 * n * total_rows * depth * local,
            bytes_accessed=n * depth * local * 2 + total_rows * local * 8,
            transcendentals=0,
        ),
    )(position, *operands)


def delta_kernel(exits, scale, logits_ref, teacher_ref, norm_ref, delta_ref, div_ref):
    b = pl.program_id(0)

    @pl.when(b == 0)
    def _():
        div_ref[...] = jnp.zeros_like(div_ref)

    rows = logits_ref.shape[0]
    tokens = rows // exits
    line = jnp.broadcast_to(norm_ref[pl.ds(b, 1), :], (LANES, LANES))
    column = line.T[:rows, :1]
    teacher = teacher_ref[0]
    target = jnp.exp(teacher)
    for e in range(exits):
        part = pl.ds(e * tokens, tokens)
        shifted = logits_ref[part, :] - column[e * tokens : (e + 1) * tokens]
        delta_ref[part, :] = ((jnp.exp(shifted) - target) * scale).astype(BF16)
        gap = jnp.sum(target * (teacher - shifted), axis=0, keepdims=True)
        gap = jnp.sum(gap, axis=1, keepdims=True)
        div_ref[pl.ds(e, 1), :] += jnp.broadcast_to(gap, (1, LANES))


def delta_pass(logits, teacher, log_total, exits, scale):
    total_rows, local = logits.shape
    n_blocks, tokens, _ = teacher.shape
    rows = exits * tokens
    return pl.pallas_call(
        functools.partial(delta_kernel, exits, scale),
        grid=(n_blocks,),
        in_specs=[
            pl.BlockSpec((rows, local), lambda b: (b, 0)),
            pl.BlockSpec((1, tokens, local), lambda b: (b, 0, 0)),
            pl.BlockSpec((n_blocks, LANES), lambda b: (0, 0)),
        ],
        out_specs=[
            pl.BlockSpec((rows, local), lambda b: (b, 0)),
            pl.BlockSpec((8, LANES), lambda b: (0, 0)),
        ],
        out_shape=[
            jax.ShapeDtypeStruct((total_rows, local), BF16),
            jax.ShapeDtypeStruct((8, LANES), F32),
        ],
        compiler_params=pltpu.CompilerParams(vmem_limit_bytes=16 << 20),
        cost_estimate=pl.CostEstimate(
            flops=total_rows * local * 8,
            bytes_accessed=total_rows * local * 6 + n_blocks * tokens * local * 4,
            transcendentals=total_rows * local,
        ),
        name="delta",
    )(logits, teacher, log_total)


def state_grad_kernel(n_blocks, n_after, *refs):
    delta_ref, weight_ref = refs[1:3]
    keep_ref, send_ref = refs[3 + n_after :]
    rows = delta_ref.shape[0] // n_blocks
    part = lax.dot_general(
        delta_ref[...], weight_ref[...], (((1,), (1,)), ((), ())), preferred_element_type=F32
    ).astype(BF16)
    for b in range(n_blocks):
        target = send_ref if b & 1 else keep_ref
        target[b >> 1] = part[b * rows : (b + 1) * rows]


def state_grad(offset, position, delta, weight, n_blocks, sections, after):
    total_rows, local = delta.shape
    rows = total_rows // n_blocks
    depth = weight.shape[0] // sections
    tile = min(512, depth)
    steps = depth // tile
    spec = pl.BlockSpec((n_blocks // 2, rows, tile), lambda i, pos: (0, 0, i))
    shape = jax.ShapeDtypeStruct((n_blocks // 2, rows, depth), BF16)
    return pl.pallas_call(
        functools.partial(state_grad_kernel, n_blocks, len(after)),
        grid_spec=pltpu.PrefetchScalarGridSpec(
            num_scalar_prefetch=1,
            grid=(steps,),
            in_specs=[
                pl.BlockSpec(
                    (total_rows, local), lambda i, pos: (0, 0), pipeline_mode=pl.Buffered(1)
                ),
                pl.BlockSpec((tile, local), lambda i, pos: (pos[offset] * steps + i, 0)),
            ]
            + [pl.BlockSpec(memory_space=pl.ANY)] * len(after),
            out_specs=[spec, spec],
        ),
        out_shape=[shape, shape],
        compiler_params=pltpu.CompilerParams(vmem_limit_bytes=24 << 20),
        cost_estimate=pl.CostEstimate(
            flops=2 * total_rows * depth * local,
            bytes_accessed=depth * (local + total_rows) * 2 + total_rows * local * 2,
            transcendentals=0,
        ),
    )(position, delta, weight, *after)


def head_grad_kernel(*refs):
    states_ref, delta_ref = refs[1:3]
    refs[-1][...] = lax.dot_general(
        states_ref[0], delta_ref[...], (((0,), (0,)), ((), ())), preferred_element_type=F32
    ).astype(BF16)


def head_grad(offset, position, states, index, delta, out, after, sections):
    _, total_rows, depth = states.shape
    local = delta.shape[1]
    tile = min(512, depth)
    steps = depth // tile
    extra = list(after) + ([] if out is None else [out])
    return pl.pallas_call(
        head_grad_kernel,
        grid_spec=pltpu.PrefetchScalarGridSpec(
            num_scalar_prefetch=1,
            grid=(steps,),
            in_specs=[
                pl.BlockSpec((1, total_rows, tile), lambda i, pos: (index, 0, i)),
                pl.BlockSpec(
                    (total_rows, local), lambda i, pos: (0, 0), pipeline_mode=pl.Buffered(1)
                ),
            ]
            + [pl.BlockSpec(memory_space=pl.ANY)] * len(extra),
            out_specs=pl.BlockSpec((tile, local), lambda i, pos: (pos[offset] * steps + i, 0)),
        ),
        out_shape=jax.ShapeDtypeStruct((sections * depth, local), BF16),
        input_output_aliases={} if out is None else {2 + len(extra): 0},
        compiler_params=pltpu.CompilerParams(vmem_limit_bytes=24 << 20),
        cost_estimate=pl.CostEstimate(
            flops=2 * total_rows * depth * local,
            bytes_accessed=depth * (local + total_rows) * 2 + total_rows * local * 2,
            transcendentals=0,
        ),
    )(position, states, delta, *extra)


def body(sections, vocabs, exit_hidden, norm_gain, head_weight, teacher):
    chips = vocabs // 2
    exits, tokens, depth = exit_hidden.shape
    rows = exits * tokens
    local = head_weight.shape[1]
    width = depth * sections
    all_tokens = tokens * vocabs
    section = lax.axis_index("section")
    vocab = lax.axis_index("vocab")
    position = jnp.stack([section ^ o for o in range(sections)]).astype(jnp.int32)

    def sec(x, mask):
        return swap(x, "section", mask, sections)

    def voc(x, mask):
        return swap(x, "vocab", mask, vocabs)

    def sec_sum(x):
        return functools.reduce(jnp.add, [x] + [sec(x, o) for o in range(1, sections)])

    hidden = exit_hidden.astype(F32)
    gains = norm_gain[:, None, :]
    squares = sec_sum(jnp.sum(hidden * hidden, axis=-1))
    inverse = lax.rsqrt(squares / width + epsilon)[..., None]
    normed = (hidden * inverse * gains).astype(BF16).reshape(rows, depth)

    order = sorted(range(sections), key=lambda o: (o.bit_count(), o))
    mine = [[None] * chips for _ in range(sections)]
    theirs = [[None] * chips for _ in range(sections)]
    mine[0][0] = normed
    sequence = gather_order(sections, chips)
    late = [step for step in sequence if step[0] == "s" and step[1].bit_count() > 1]
    late = [step for step in late if step[2] >= chips // 2]

    def gather(kind, o, k, token=None):
        if kind == "z":
            source, bit = mine[0][k ^ low(k)], low(k)
        else:
            bit = route(o, k)
            source = mine[o ^ bit][k]
        if token is not None:
            source, _ = lax.optimization_barrier((source, token))
        mine[o][k] = voc(source, 2 * bit) if kind == "z" else sec(source, bit)

    for step in sequence:
        if step not in late:
            gather(*step)
    for k in range(chips):
        theirs[0][k] = voc(mine[0][k], 1)

    def column_block(mask):
        return lax.dynamic_slice_in_dim(teacher, (vocab ^ mask) * local, local, axis=1)

    keep = [column_block(2 * k) for k in range(chips)]
    other = voc(jnp.stack([column_block(2 * k + 1) for k in range(chips)]), 1)
    teacher_blocks = [jnp.stack([keep[0], other[0]])]
    for k in range(1, chips):
        pair = jnp.stack([keep[k], other[k]])
        pair, _ = lax.optimization_barrier((pair, mine[0][-1]))
        teacher_blocks.append(voc(pair, 2 * k))
    teacher_cols = jnp.concatenate(teacher_blocks, axis=0)

    groups = []
    for o in order:
        if groups and groups[-1][0].bit_count() == o.bit_count():
            groups[-1].append(o)
        else:
            groups.append([o])
    acc, states = None, {}
    for index, group in enumerate(groups):
        pieces = [
            [(theirs if b & 1 else mine)[o][b >> 1] for b in range(vocabs)] for o in group
        ]
        result = logits_part(
            group, position, pieces, head_weight, acc, index == len(groups) - 1
        )
        acc, block_states, stats = result
        for g, o in enumerate(group):
            states[o] = (block_states, g)
        if index == 0:
            for step in late:
                gather(*step, token=stats)
            for o in order[1:]:
                for k in range(chips):
                    block, _ = lax.optimization_barrier((mine[o][k], stats))
                    theirs[o][k] = voc(block, 1)
    logits = acc

    others = [sec(stats, o) for o in range(1, sections)]
    stats = merge(stats, others, [0] * len(others))
    others = [voc(stats, 2 * k) for k in range(1, chips)]
    stats = merge(stats, others, [2 * k for k in range(1, chips)])
    log_total = merge(stats, [voc(stats, 1)], [1], log=True)

    delta, gaps = delta_pass(logits, teacher_cols, log_total, exits, loss_scale / all_tokens)

    kept, got, moved = {}, {}, {}

    def total_of(o, k):
        total = kept[o][k].astype(F32) + got[o][k].astype(F32)
        for block in moved.get((o, k), ()):
            total = total + block.astype(F32)
        return total

    def send(todo):
        packed = [total_of(o, k).astype(BF16) for o, k in todo]
        for (o, k), block in zip(todo, packed):
            bit = route(o, k)
            moved.setdefault((o ^ bit, k), []).append(sec(block, bit))
        return packed

    backward = list(reversed(order))
    sends = reduce_order(sections, chips)
    first = [step for step in sends if step[0] == backward[0]]
    after = []
    for index, o in enumerate(backward):
        kept[o], sent = state_grad(o, position, delta, head_weight, vocabs, sections, after)
        got[o] = voc(sent, 1)
        after = [kept[o]]
        if index == 1:
            after += send(first)
    rest = [step for step in sends if step not in first]
    for count in range(sections.bit_length() - 1, 0, -1):
        for k in reversed(range(chips)):
            after += send([step for step in rest if step[0].bit_count() == count and step[1] == k])

    sums = {}
    chain = []
    for k in range(chips - 1, 0, -1):
        total = sums.pop(k, 0.0) + total_of(0, k)
        packed = total.astype(BF16)
        chain.append(packed)
        sums[k ^ low(k)] = sums.get(k ^ low(k), 0.0) + voc(packed, 2 * low(k)).astype(F32)
    own_sum = sums[0] + total_of(0, 0)

    share = -(-len(chain) // (sections - 1))
    grad_head = None
    for o in range(sections):
        if o:
            after = chain[(o - 1) * share : o * share]
        block_states, index = states[o]
        grad_head = head_grad(
            o, position, block_states, index, delta, grad_head, after, sections
        )

    gap = gaps[:, :1].reshape(1, 8)
    for index in range(vocabs.bit_length() - 1):
        gap, _ = lax.optimization_barrier((gap, chain[min(index, len(chain) - 1)]))
        gap = gap + voc(gap, 1 << index)

    grad_normed = own_sum.reshape(exits, tokens, depth)
    weighted = gains * grad_normed
    inner = jnp.sum(weighted * hidden, axis=-1)
    gap_row = jnp.pad(gap[:, :exits], ((0, 0), (0, tokens - exits)))
    joined = sec_sum(jnp.concatenate([inner, gap_row], axis=0))
    divergence = joined[exits, :exits] / all_tokens
    inner = joined[:exits][..., None]
    grad_hidden = (inverse * weighted - hidden * inverse**3 * inner / width).astype(BF16)
    return divergence, grad_hidden, grad_head


def solution(mesh):
    sections, vocabs = mesh.shape["section"], mesh.shape["vocab"]
    return jax.shard_map(
        functools.partial(body, sections, vocabs),
        mesh=mesh,
        in_specs=(
            P(None, "vocab", "section"),
            P(None, "section"),
            P(None, ("section", "vocab")),
            P("vocab", "section"),
        ),
        out_specs=(P(), P(None, "vocab", "section"), P(None, ("section", "vocab"))),
        check_vma=False,
    )
```

```python
import functools
import jax
import jax.numpy as jnp
from jax import lax
from jax.experimental import pallas as pl
from jax.experimental.pallas import tpu as pltpu
from jax.sharding import PartitionSpec as P

epsilon = 1e-05
loss_scale = 1024.0
F32 = jnp.float32
BF16 = jnp.bfloat16
LANES = 128


def swap(x, axis, mask, size):
    return lax.ppermute(x, axis, [(i, i ^ mask) for i in range(size)])


def low(o):
    return o & -o


def high(o):
    return 1 << (o.bit_length() - 1)


def route(o, k):
    return low(o) if k & 1 else high(o)


def gather_order(sections, chips):
    single = [o for o in range(1, sections) if o.bit_count() == 1]
    several = sorted(
        (o for o in range(1, sections) if o.bit_count() > 1), key=lambda o: (o.bit_count(), o)
    )
    seq = []
    for k in range(chips + 1):
        if k < chips:
            seq += [("z", 0, c) for c in range(1, chips) if c ^ low(c) == k]
            seq += [("s", o, k) for o in single]
        if k:
            seq += [("s", o, k - 1) for o in several]
    return seq


def merge_kernel(masks, log, *refs):
    own, others, out = refs[0], refs[1:-1], refs[-1]
    n = own.shape[1]
    for b in range(n):
        row = pl.ds(b, 1)
        sources = [(own, row)] + [(r, pl.ds(b ^ m, 1)) for r, m in zip(others, masks)]
        tops = [r[0, at, :] for r, at in sources]
        top = functools.reduce(jnp.maximum, tops)
        total = functools.reduce(
            jnp.add, [r[1, at, :] * jnp.exp(t - top) for (r, at), t in zip(sources, tops)]
        )
        if log:
            out[row, :] = top + jnp.log(total)
        else:
            out[0, row, :] = top
            out[1, row, :] = total


def merge(own, others, masks, log=False):
    return pl.pallas_call(
        functools.partial(merge_kernel, masks, log),
        out_shape=jax.ShapeDtypeStruct(own.shape[1:] if log else own.shape, F32),
        compiler_params=pltpu.CompilerParams(vmem_limit_bytes=4 << 20),
        name="merge",
    )(own, *others)


def own_kernel(*refs):
    mine_ref, theirs_ref, weight_ref, out_ref = refs[1:]
    chips, rows, depth = mine_ref.shape
    states = jnp.concatenate(
        [mine_ref[...].reshape(chips * rows, depth), theirs_ref[...].reshape(chips * rows, depth)],
        axis=0,
    )
    out_ref[...] = jnp.dot(states, weight_ref[...], preferred_element_type=F32)


def own_pass(position, mine, theirs, weight):
    chips, rows, depth = mine.shape
    total_rows = 2 * chips * rows
    local = weight.shape[1]
    tile = min(512, local)
    piece = pl.BlockSpec(
        (chips, rows, depth), lambda i, pos: (0, 0, 0), pipeline_mode=pl.Buffered(1)
    )
    return pl.pallas_call(
        own_kernel,
        grid_spec=pltpu.PrefetchScalarGridSpec(
            num_scalar_prefetch=1,
            grid=(local // tile,),
            in_specs=[piece, piece, pl.BlockSpec((depth, tile), lambda i, pos: (pos[0], i))],
            out_specs=pl.BlockSpec((total_rows, tile), lambda i, pos: (0, i)),
        ),
        out_shape=jax.ShapeDtypeStruct((total_rows, local), F32),
        compiler_params=pltpu.CompilerParams(vmem_limit_bytes=24 << 20),
        cost_estimate=pl.CostEstimate(
            flops=2 * total_rows * depth * local,
            bytes_accessed=depth * (local + total_rows) * 2 + total_rows * local * 4,
            transcendentals=0,
        ),
        name="own_part",
    )(position, mine, theirs, weight)


def logits_kernel(offsets, chips, *refs):
    n = len(offsets)
    pieces, refs = refs[1 : 1 + 2 * n], refs[1 + 2 * n :]
    weights, refs = refs[:n], refs[n:]
    own_ref, out_ref, stat_ref, lhs, max_ref, sum_ref, even_ref, odd_ref, sem = refs
    rows = pieces[0].shape[1]
    step = pl.program_id(0)
    every = [(c, k) for c in range(2) for k in range(chips)]

    def incoming(g, c, k):
        return pltpu.make_async_copy(
            pieces[2 * g + c].at[k],
            lhs.at[g, pl.ds((c * chips + k) * rows, rows), :],
            sem.at[g, c, k],
        )

    columns = range(0, out_ref.shape[1], LANES)

    def absorb(held):
        for b in range(2 * chips):
            at = pl.ds(b * rows, rows)
            old = max_ref[at, :]
            new = functools.reduce(jnp.maximum, [held[at, pl.ds(c, LANES)] for c in columns], old)
            fresh = functools.reduce(
                jnp.add, [jnp.exp(held[at, pl.ds(c, LANES)] - new) for c in columns]
            )
            sum_ref[at, :] = sum_ref[at, :] * jnp.exp(old - new) + fresh
            max_ref[at, :] = new

    @pl.when(step == 0)
    def _():
        for g in range(n):
            for c, k in every:
                incoming(g, c, k).start()
        even_ref[...] = own_ref[...]
        for g in range(n):
            for c, k in every:
                incoming(g, c, k).wait()
            even_ref[...] += jnp.dot(lhs[g], weights[g][...], preferred_element_type=F32)
        out_ref[...] = even_ref[...]
        max_ref[...] = even_ref[:, :LANES]
        sum_ref[...] = jnp.zeros_like(sum_ref)

    for odd, (now, before) in enumerate(((even_ref, odd_ref), (odd_ref, even_ref))):

        @pl.when((step > 0) & (step % 2 == odd))
        def _():
            block = own_ref[...]
            for g in range(n):
                block += jnp.dot(lhs[g], weights[g][...], preferred_element_type=F32)
            absorb(before)
            out_ref[...] = block
            now[...] = block

    @pl.when(step == pl.num_programs(0) - 1)
    def _():
        absorb(out_ref)
        pad = jnp.ones((LANES - rows, LANES), F32)
        for b in range(2 * chips):
            at = pl.ds(b * rows, rows)
            top = jnp.max(max_ref[at, :], axis=1, keepdims=True)
            total = jnp.sum(sum_ref[at, :] * jnp.exp(max_ref[at, :] - top), axis=1, keepdims=True)
            for plane, value in enumerate((top, total)):
                tile = jnp.concatenate([jnp.broadcast_to(value, (rows, LANES)), pad], axis=0)
                stat_ref[plane, pl.ds(b, 1), :] = tile.T[:1, :]


def logits_pass(offsets, position, pieces, weight, own):
    n = len(offsets)
    chips, _, depth = pieces[0].shape
    total_rows, local = own.shape
    tile = min(256, local)
    stats = (2, 2 * chips, LANES)
    block = pl.BlockSpec((total_rows, tile), lambda i, pos: (0, i))

    def weight_spec(offset):
        return pl.BlockSpec((depth, tile), lambda i, pos: (pos[offset], i))

    return pl.pallas_call(
        functools.partial(logits_kernel, offsets, chips),
        grid_spec=pltpu.PrefetchScalarGridSpec(
            num_scalar_prefetch=1,
            grid=(local // tile,),
            in_specs=[pl.BlockSpec(memory_space=pl.ANY)] * (2 * n)
            + [weight_spec(o) for o in offsets]
            + [block],
            out_specs=[block, pl.BlockSpec(stats, lambda i, pos: (0, 0, 0))],
            scratch_shapes=[
                pltpu.VMEM((n, total_rows, depth), BF16),
                pltpu.VMEM((total_rows, LANES), F32),
                pltpu.VMEM((total_rows, LANES), F32),
                pltpu.VMEM((total_rows, tile), F32),
                pltpu.VMEM((total_rows, tile), F32),
                pltpu.SemaphoreType.DMA((n, 2, chips)),
            ],
        ),
        out_shape=[
            jax.ShapeDtypeStruct((total_rows, local), F32),
            jax.ShapeDtypeStruct(stats, F32),
        ],
        compiler_params=pltpu.CompilerParams(vmem_limit_bytes=29 << 20),
        cost_estimate=pl.CostEstimate(
            flops=2 * total_rows * n * depth * local,
            bytes_accessed=n * depth * (local + total_rows) * 2 + total_rows * local * 8,
            transcendentals=total_rows * local,
        ),
        name="logits",
    )(position, *pieces, *[weight] * n, own)


def delta_kernel(exits, scale, chips, logits_ref, norm_ref, *refs):
    teachers, (delta_ref, div_ref) = refs[:chips], refs[chips:]
    b = pl.program_id(0)

    @pl.when(b == 0)
    def _():
        div_ref[...] = jnp.zeros_like(div_ref)

    rows = logits_ref.shape[0]
    tokens = rows // exits
    for k in range(chips):

        @pl.when(b % chips == k)
        def _():
            line = jnp.broadcast_to(norm_ref[pl.ds(b, 1), :], (LANES, LANES))
            column = line.T[:rows, :1]
            teacher = teachers[k][b // chips]
            target = jnp.exp(teacher)
            for e in range(exits):
                part = pl.ds(e * tokens, tokens)
                shifted = logits_ref[part, :] - column[e * tokens : (e + 1) * tokens]
                delta_ref[part, :] = ((jnp.exp(shifted) - target) * scale).astype(BF16)
                gap = jnp.sum(target * (teacher - shifted), axis=0, keepdims=True)
                gap = jnp.sum(gap, axis=1, keepdims=True)
                div_ref[pl.ds(e, 1), :] += jnp.broadcast_to(gap, (1, LANES))


def delta_pass(logits, teachers, log_total, exits, scale):
    total_rows, local = logits.shape
    chips = len(teachers)
    tokens = teachers[0].shape[1]
    n_blocks = 2 * chips
    rows = exits * tokens
    pair = pl.BlockSpec(
        (2, tokens, local), lambda b: (0, 0, 0), pipeline_mode=pl.Buffered(1)
    )
    return pl.pallas_call(
        functools.partial(delta_kernel, exits, scale, chips),
        grid=(n_blocks,),
        in_specs=[
            pl.BlockSpec((rows, local), lambda b: (b, 0)),
            pl.BlockSpec((n_blocks, LANES), lambda b: (0, 0)),
        ]
        + [pair] * chips,
        out_specs=[
            pl.BlockSpec((rows, local), lambda b: (b, 0)),
            pl.BlockSpec((8, LANES), lambda b: (0, 0)),
        ],
        out_shape=[
            jax.ShapeDtypeStruct((total_rows, local), BF16),
            jax.ShapeDtypeStruct((8, LANES), F32),
        ],
        compiler_params=pltpu.CompilerParams(vmem_limit_bytes=9 << 20),
        cost_estimate=pl.CostEstimate(
            flops=total_rows * local * 8,
            bytes_accessed=total_rows * local * 6 + n_blocks * tokens * local * 4,
            transcendentals=total_rows * local,
        ),
        name="delta",
    )(logits, log_total, *teachers)


def state_grad_kernel(n_after, *refs):
    delta_ref, weight_ref = refs[1:3]
    keep_ref, send_ref = refs[3 + n_after :]
    chips, rows = keep_ref.shape[1:3]
    part = lax.dot_general(
        delta_ref[...], weight_ref[...], (((1,), (1,)), ((), ())), preferred_element_type=F32
    ).astype(BF16)
    for k in range(chips):
        keep_ref[0, k] = part[k * rows : (k + 1) * rows]
        send_ref[0, k] = part[(chips + k) * rows : (chips + k + 1) * rows]


def state_grad(places, delta, weight, chips, sections, after):
    n = places.shape[0]
    total_rows, local = delta.shape
    rows = total_rows // (2 * chips)
    depth = weight.shape[0] // sections
    tile = min(512, depth)
    steps = depth // tile
    spec = pl.BlockSpec((1, chips, rows, tile), lambda g, i, pos: (g, 0, 0, i))
    shape = jax.ShapeDtypeStruct((n, chips, rows, depth), BF16)
    return pl.pallas_call(
        functools.partial(state_grad_kernel, len(after)),
        grid_spec=pltpu.PrefetchScalarGridSpec(
            num_scalar_prefetch=1,
            grid=(n, steps),
            in_specs=[
                pl.BlockSpec(
                    (total_rows, local), lambda g, i, pos: (0, 0), pipeline_mode=pl.Buffered(1)
                ),
                pl.BlockSpec((tile, local), lambda g, i, pos: (pos[g] * steps + i, 0)),
            ]
            + [pl.BlockSpec(memory_space=pl.ANY)] * len(after),
            out_specs=[spec, spec],
        ),
        out_shape=[shape, shape],
        compiler_params=pltpu.CompilerParams(vmem_limit_bytes=17 << 20),
        cost_estimate=pl.CostEstimate(
            flops=2 * n * total_rows * depth * local,
            bytes_accessed=n * depth * (local + total_rows) * 2 + total_rows * local * 2,
            transcendentals=0,
        ),
        name="to_states",
    )(places, delta, weight, *after)


def head_grad_kernel(n, steps, *refs):
    delta_ref = refs[1 + 2 * n]
    step = pl.program_id(0)
    chips, rows, tile = refs[1].shape
    for g in range(n):
        mine_ref, theirs_ref = refs[1 + 2 * g : 3 + 2 * g]

        @pl.when((step >= g * steps) & (step < (g + 1) * steps))
        def _():
            states = jnp.concatenate(
                [
                    mine_ref[...].reshape(chips * rows, tile),
                    theirs_ref[...].reshape(chips * rows, tile),
                ],
                axis=0,
            )
            refs[-1][...] = lax.dot_general(
                states, delta_ref[...], (((0,), (0,)), ((), ())), preferred_element_type=F32
            ).astype(BF16)


def head_grad(places, states, delta, out, after, sections):
    n = len(states)
    chips, rows, depth = states[0][0].shape
    total_rows, local = delta.shape
    tile = min(512, depth)
    steps = depth // tile
    extra = list(after) + ([] if out is None else [out])

    def piece(g):
        return pl.BlockSpec(
            (chips, rows, tile), lambda i, pos: (0, 0, jnp.clip(i - g * steps, 0, steps - 1))
        )

    return pl.pallas_call(
        functools.partial(head_grad_kernel, n, steps),
        grid_spec=pltpu.PrefetchScalarGridSpec(
            num_scalar_prefetch=1,
            grid=(n * steps,),
            in_specs=[piece(g) for g in range(n) for _ in range(2)]
            + [
                pl.BlockSpec(
                    (total_rows, local), lambda i, pos: (0, 0), pipeline_mode=pl.Buffered(1)
                ),
            ]
            + [pl.BlockSpec(memory_space=pl.ANY)] * len(extra),
            out_specs=pl.BlockSpec(
                (tile, local), lambda i, pos: (pos[i // steps] * steps + i % steps, 0)
            ),
        ),
        out_shape=jax.ShapeDtypeStruct((sections * depth, local), BF16),
        input_output_aliases={} if out is None else {1 + 2 * n + len(extra): 0},
        compiler_params=pltpu.CompilerParams(vmem_limit_bytes=17 << 20),
        cost_estimate=pl.CostEstimate(
            flops=2 * n * total_rows * depth * local,
            bytes_accessed=n * depth * (local + total_rows) * 2 + total_rows * local * 2,
            transcendentals=0,
        ),
        name="to_head",
    )(places, *[block for pair in states for block in pair], delta, *extra)


def send_groups(sections, chips):
    groups = []
    half = chips // 2
    for count in range(sections.bit_length() - 1, 0, -1):
        offsets = [o for o in range(1, sections) if o.bit_count() == count]
        if count > 1:
            parts = [tuple(k for k in reversed(range(chips)) if k & 1 == odd) for odd in (1, 0)]
        else:
            parts = [(k,) for k in reversed(range(half, chips))]
            parts.append(tuple(reversed(range(half))))
        groups += [(o, ks) for ks in parts for o in offsets]
    return groups


def body(sections, vocabs, exit_hidden, norm_gain, head_weight, teacher):
    chips = vocabs // 2
    exits, tokens, depth = exit_hidden.shape
    rows = exits * tokens
    local = head_weight.shape[1]
    width = depth * sections
    all_tokens = tokens * vocabs
    section = lax.axis_index("section")
    vocab = lax.axis_index("vocab")
    position = jnp.stack([section ^ o for o in range(sections)]).astype(jnp.int32)

    def sec(x, mask):
        return swap(x, "section", mask, sections)

    def voc(x, mask):
        return swap(x, "vocab", mask, vocabs)

    def sec_sum(x):
        parts = [x]
        for o in range(1, sections):
            parts.append(sec(x, o))
        return functools.reduce(jnp.add, parts)

    order = sorted(range(sections), key=lambda o: (o.bit_count(), o))
    mine = [[None] * chips for _ in range(sections)]
    mine[0][0] = exit_hidden.reshape(rows, depth)
    for kind, o, k in gather_order(sections, chips):
        if kind == "z":
            mine[o][k] = voc(mine[0][k ^ low(k)], 2 * low(k))
        else:
            bit = route(o, k)
            mine[o][k] = sec(mine[o ^ bit][k], bit)

    hidden = exit_hidden.astype(F32)
    gains = norm_gain[:, None, :]
    squares = sec_sum(jnp.sum(hidden * hidden, axis=-1))
    inverse = lax.rsqrt(squares / width + epsilon)
    inverses = [inverse] + [voc(inverse, 2 * k) for k in range(1, chips)]
    inverse = inverse[..., None]
    normed, theirs, last = [None] * sections, [None] * sections, None
    for o in order:
        gain = (sec(norm_gain, o) if o else norm_gain)[:, None, :]
        raw = mine[o]
        if last is not None:
            *raw, _ = lax.optimization_barrier((*raw, last))
        blocks = [
            (raw[k].reshape(exits, tokens, depth).astype(F32) * inverses[k][..., None] * gain)
            .astype(BF16)
            .reshape(rows, depth)
            for k in range(chips)
        ]
        last = normed[o] = jnp.stack(blocks)
        theirs[o] = voc(normed[o], 1)

    def column_block(mask):
        return lax.dynamic_slice_in_dim(teacher, (vocab ^ mask) * local, local, axis=1)

    keep = [column_block(2 * k) for k in range(chips)]
    other = voc(jnp.stack([column_block(2 * k + 1) for k in range(chips)]), 1)
    teachers = [jnp.stack([keep[0], other[0]])]
    for k in range(1, chips):
        pair = jnp.stack([keep[k], other[k]])
        pair, _ = lax.optimization_barrier((pair, mine[0][-1]))
        teachers.append(voc(pair, 2 * k))

    own = own_pass(position, normed[0], theirs[0], head_weight)
    pieces = [block for o in order[1:] for block in (normed[o], theirs[o])]
    logits, stats = logits_pass(order[1:], position, pieces, head_weight, own)
    others = [sec(stats, o) for o in range(1, sections)]
    stats = merge(stats, others, [0] * len(others))
    others = [voc(stats, 2 * k) for k in range(1, chips)]
    stats = merge(stats, others, list(range(1, chips)))
    log_total = merge(stats, [voc(stats, 1)], [chips], log=True)

    delta, gaps = delta_pass(logits, teachers, log_total, exits, loss_scale / all_tokens)

    kept, got, moved = {}, {}, {}

    def places(offsets):
        return jnp.stack([section ^ o for o in offsets]).astype(jnp.int32)

    def total_of(o, k, token=None):
        blocks = [kept[o][k], got[o][k], *moved.get((o, k), ())]
        if token is not None:
            *blocks, _ = lax.optimization_barrier((*blocks, token))
        return functools.reduce(jnp.add, [block.astype(F32) for block in blocks])

    def send(o, ks):
        packed = {}
        for bit in sorted({route(o, k) for k in ks}):
            group = [k for k in ks if route(o, k) == bit]
            packed[bit] = jnp.stack([total_of(o, k).astype(BF16) for k in group])
            arrived = sec(packed[bit], bit)
            for i, k in enumerate(group):
                moved.setdefault((o ^ bit, k), []).append(arrived[i])
        return list(packed.values())

    groups = send_groups(sections, chips)
    backward = list(reversed(order))
    levels = [[o] for o in backward]
    after = []
    for index, level in enumerate(levels):
        kept_level, sent = state_grad(
            places(level), delta, head_weight, chips, sections, after
        )
        got_level = voc(sent, 1)
        for g, o in enumerate(level):
            kept[o], got[o] = kept_level[g], got_level[g]
        after = [kept_level]
        if index == 1:
            for group in groups:
                if group[0] == sections - 1:
                    after += send(*group)
    for group in groups:
        if group[0] != sections - 1:
            after += send(*group)

    sums = {}
    chain = []
    for k in range(chips - 1, 0, -1):
        total = sums.pop(k, 0.0) + total_of(0, k, chain[-1] if chain else None)
        packed = total.astype(BF16)
        chain.append(packed)
        arrived = voc(packed, 2 * low(k))
        sums[k ^ low(k)] = sums.get(k ^ low(k), 0.0) + arrived.astype(F32)
    own_sum = sums[0] + total_of(0, 0)

    calls = [[o] for o in range(sections)]
    share = -(-len(chain) // (len(calls) - 1))
    grad_head = None
    for index, offsets in enumerate(calls):
        if index:
            after = chain[(index - 1) * share : index * share]
        grad_head = head_grad(
            places(offsets), [(normed[o], theirs[o]) for o in offsets],
            delta, grad_head, after, sections,
        )

    gap = gaps[:, :1].reshape(1, 8)
    gates = [kept[0], *chain]
    for index in range(vocabs.bit_length() - 1):
        gap, _ = lax.optimization_barrier((gap, gates[min(index, len(gates) - 1)]))
        gap = gap + voc(gap, 1 << index)

    grad_normed = own_sum.reshape(exits, tokens, depth)
    weighted = gains * grad_normed
    inner = jnp.sum(weighted * hidden, axis=-1)
    gap_row = jnp.pad(gap[:, :exits], ((0, 0), (0, tokens - exits)))
    joined = sec_sum(jnp.concatenate([inner, gap_row], axis=0))
    divergence = joined[exits, :exits] / all_tokens
    inner = joined[:exits][..., None]
    grad_hidden = (inverse * weighted - hidden * inverse**3 * inner / width).astype(BF16)
    return divergence, grad_hidden, grad_head


def solution(mesh):
    sections, vocabs = mesh.shape["section"], mesh.shape["vocab"]
    return jax.shard_map(
        functools.partial(body, sections, vocabs),
        mesh=mesh,
        in_specs=(
            P(None, "vocab", "section"),
            P(None, "section"),
            P(None, ("section", "vocab")),
            P("vocab", "section"),
        ),
        out_specs=(P(), P(None, "vocab", "section"), P(None, ("section", "vocab"))),
        check_vma=False,
    )
```
